256 devices in a mesh: worker: 16 (over x_lo, y, core), shard: 16 (over z, x_hi).
Axes of the slice: x: 4 (x_hi: 2, x_lo: 2; x = x_hi * 2 + x_lo), y: 4, z: 8, core: 2. Of those that a mesh axis runs over, the one named last changes fastest.
Arguments:
- momentum: float32 [16, 8388608], P('worker', 'shard'), may hold values from -6 to 6
- gradient: float32 [16, 8388608], P('worker', 'shard'), may hold values from -40 to 40
- weights: float32 [8388608], P('shard'), may hold values from -0.6 to 0.6
Outputs:
- new_momentum: float32 [16, 8388608], P('worker', 'shard')
- new_weights: float32 [8388608], P('shard')
The draws below stay inside these ranges and needn't reach their ends.
All inputs are finite; a program needn't handle non-finite values.
Results may differ from the reference program's by a relative error of at most 0.0003.
Values sent between devices are 32-bit elements; how exact they have to be, the bound alone decides.
A program may use at most 64 MiB of HBM per device.

```python
import jax
import jax.numpy as jnp

WORKERS = 16
TRIM = 4
P_SIZE = 8388608


def draw_gradient(key, part):
    keys = jax.random.split(jax.random.fold_in(key, 7), 6)
    shape = (WORKERS, P_SIZE)
    honest = jax.random.normal(keys[2], shape, dtype=jnp.float32)
    share = 0.2
    sizes = jax.random.uniform(keys[3], shape, dtype=jnp.float32, minval=10.0, maxval=30.0)
    signs = jnp.where(jax.random.uniform(keys[4], (1, P_SIZE), dtype=jnp.float32) < 0.5, -1.0, 1.0)
    attack = jax.random.uniform(keys[5], shape, dtype=jnp.float32) < share
    result = jnp.where(attack, signs * sizes, honest)
    return jnp.clip(result, -40.0, 40.0).astype(jnp.float32)


def levels(stream_key, extent, pieces, least, largest):
    loudness, own = 1.0, jax.random.fold_in(stream_key, 6)
    for dim, blocks in pieces:
        draws = jnp.exp(jax.random.uniform(jax.random.fold_in(own, dim), (blocks,), jnp.float32, least / len(pieces), largest / len(pieces)))
        loudness = loudness * jnp.repeat(draws, extent[dim] // blocks).reshape([-1 if axis == dim else 1 for axis in range(len(extent))])
    return loudness


def bell_draw(key, shape, width, most, shards=(), kind=jnp.bfloat16):
    values = jax.random.normal(key, shape, jnp.float32) * width
    if len(shards) > 0:
        values = levels(key, shape, shards, -0.22, 0.18) * values
    return jnp.clip(values, min=-most, max=most).astype(kind)


def setup_inputs(seed: int = 0) -> dict:
    splits = jax.random.split(jax.random.key(seed), 4)
    return {
        "momentum": bell_draw(splits[0], (WORKERS, P_SIZE), 1.0, 6.0, ((0, 16), (1, 16)), jnp.float32),
        "gradient": draw_gradient(jax.random.fold_in(splits[3], 71), 0),
        "weights": bell_draw(splits[2], (P_SIZE,), 0.1, 0.6, ((0, 16),), jnp.float32),
    }


def reference(momentum, gradient, weights):
    new_momentum = 0.9 * momentum + gradient
    ordered = jnp.sort(new_momentum, axis=0)
    kept = ordered[TRIM:WORKERS - TRIM]
    trimmed = jnp.sum(kept, axis=0) / (WORKERS - 2 * TRIM)
    new_weights = weights - 0.1 * trimmed
    return new_momentum, new_weights
```

```python
import functools

import jax
import jax.numpy as jnp
from jax import lax
from jax.experimental import pallas as pl
from jax.experimental.pallas import tpu as pltpu
from jax.sharding import PartitionSpec as P

MESH = pl.DeviceIdType.MESH
LANES = 128
N = 16
CHUNKS = (64, 64, 64, 64)
VIA_X = (False, True, False, False)
SORT8 = (
    ((0, 2), (1, 3), (4, 6), (5, 7)),
    ((0, 4), (1, 5), (2, 6), (3, 7)),
    ((0, 1), (2, 3), (4, 5), (6, 7)),
    ((2, 4), (3, 5)),
    ((1, 4), (3, 6)),
    ((1, 2), (3, 4), (5, 6)),
)


def sort8(values):
    values = list(values)
    for layer in SORT8:
        for i, j in layer:
            a, b = values[i], values[j]
            values[i], values[j] = jnp.minimum(a, b), jnp.maximum(a, b)
    return values


def trimmed_sum(values):
    a, b = sort8(values[:8]), sort8(values[8:])
    kept = [jnp.maximum(a[i], b[3 - i]) for i in range(4)]
    kept += [jnp.minimum(a[4 + i], b[7 - i]) for i in range(4)]
    while len(kept) > 1:
        kept = [kept[i] + kept[i + 1] for i in range(0, len(kept), 2)]
    return kept[0]


def exchange(m_ref, g_ref, w_ref, upd, new_w, m_buf, g_buf, w_buf, recv,
             load_sem, w_sem, out_sem, in_sem, near_sem, far_sem, core_sem, gather_sem):
    me = lax.axis_index("worker")
    x, y, c = me // 8, (me // 2) % 4, me % 2

    def at(dx, dy, dc):
        return ((x + dx) % 2) * 8 + ((y + dy) % 4) * 2 + (c + dc) % 2

    def wait_bytes(ref, sem):
        pltpu.make_async_copy(ref, ref, sem).wait()

    def send(src, dst, s_sem, r_sem, peer):
        pltpu.make_async_remote_copy(
            src_ref=src, dst_ref=dst, send_sem=s_sem, recv_sem=r_sem,
            device_id={"worker": peer}, device_id_type=MESH,
        ).start()

    offsets = [(dx, dy, dc) for dy in (2, 1, 3, 0) for dx in (1, 0) for dc in (0, 1)]
    offsets = [o for o in offsets if o != (0, 0, 0)]
    starts = [sum(CHUNKS[:k]) for k in range(len(CHUNKS))]
    spans = [pl.ds(s, r) for s, r in zip(starts, CHUNKS)]

    barrier = pltpu.get_barrier_semaphore()
    for o in offsets:
        pl.semaphore_signal(barrier, inc=1, device_id={"worker": at(*o)}, device_id_type=MESH)
    loads = []
    for k, span in enumerate(spans):
        pair = (
            pltpu.make_async_copy(m_ref.at[:, span], m_buf.at[:, span], load_sem.at[0, k]),
            pltpu.make_async_copy(g_ref.at[:, span], g_buf.at[:, span], load_sem.at[1, k]),
        )
        for copy in pair:
            copy.start()
        loads.append(pair)
    w_load = pltpu.make_async_copy(w_ref.at[me], w_buf, w_sem)
    w_load.start()

    def update(k):
        for copy in loads[k]:
            copy.wait()

        def one(d, _):
            upd[d, spans[k], :] = 0.9 * m_buf[d, spans[k], :] + g_buf[d, spans[k], :]
            return 0

        lax.fori_loop(0, N, one, 0)
        recv[me, spans[k], :] = upd[me, spans[k], :]

    def scatter(k):
        for o in offsets:
            peer = at(*o)
            send(upd.at[peer, spans[k]], recv.at[me, spans[k]], out_sem.at[k], in_sem.at[k], peer)

    update(0)
    for k in range(len(CHUNKS)):
        if k + 1 < len(CHUNKS):
            update(k + 1)
        if k == 0:
            pl.semaphore_wait(barrier, len(offsets))
        scatter(k)
    w_load.wait()

    def gather(block, k, r_sem, peer):
        send(new_w.at[block, spans[k]], new_w.at[block, spans[k]], gather_sem.at[k], r_sem, peer)

    other_core, other_x = at(0, 0, 1), at(1, 0, 0)
    for k in range(len(CHUNKS)):
        wait_bytes(recv.at[pl.ds(0, N - 1), spans[k]], in_sem.at[k])

        def one(r, _, k=k):
            rows = pl.ds(pl.multiple_of(starts[k] + r * 8, 8), 8)
            total = trimmed_sum([recv[d, rows, :] for d in range(N)])
            new_w[me, rows, :] = w_buf[rows, :] - 0.1 * (total * 0.125)
            return 0

        lax.fori_loop(0, CHUNKS[k] // 8, one, 0)
        gather(me, k, near_sem.at[k, 0], other_x)
        for i, dy in enumerate((2, 1, 3)):
            gather(me, k, near_sem.at[k, i + 1], at(0, dy, 0))
        gather(me, k, core_sem, other_core)

    for k in range(len(CHUNKS)):
        wait_bytes(new_w.at[other_x, spans[k]], near_sem.at[k, 0])
        if not VIA_X[k]:
            gather(other_x, k, far_sem.at[k, 1], at(0, 1, 0))
            gather(other_x, k, far_sem.at[k, 2], at(0, 3, 0))
        gather(other_x, k, core_sem, other_core)
        for i, dy in enumerate((2, 1, 3)):
            block = at(0, -dy, 0)
            wait_bytes(new_w.at[block, spans[k]], near_sem.at[k, i + 1])
            if dy == 2 or VIA_X[k]:
                gather(block, k, far_sem.at[k, i], other_x)
            gather(block, k, core_sem, other_core)
    for k in range(len(CHUNKS)):
        for i, dy in enumerate((2, 1, 3)):
            block = at(1, -dy, 0)
            wait_bytes(new_w.at[block, spans[k]], far_sem.at[k, i])
            gather(block, k, core_sem, other_core)
    wait_bytes(new_w.at[pl.ds(0, 8)], core_sem)
    for k in range(len(CHUNKS)):
        wait_bytes(recv.at[pl.ds(0, N - 1), spans[k]], out_sem.at[k])
        wait_bytes(recv.at[pl.ds(0, N - 1), spans[k]], gather_sem.at[k])


def put_out(upd, new_w, upd_out, new_w_out, sems):
    parts = 4
    copies = []
    for i, (src, dst) in enumerate(((upd, upd_out), (new_w, new_w_out))):
        for p in range(parts):
            span = pl.ds(p * (N // parts), N // parts)
            copies.append(pltpu.make_async_copy(src.at[span], dst.at[span], sems.at[i, p]))
    for copy in copies:
        copy.start()
    for copy in copies:
        copy.wait()


def body(momentum, gradient, weights):
    rows = momentum.shape[1] // (N * LANES)
    shape = (N, rows, LANES)
    k = len(CHUNKS)
    any_spec = pl.BlockSpec(memory_space=pl.ANY)
    upd, new_w = pl.pallas_call(
        exchange,
        out_shape=(pltpu.VMEM(shape, jnp.float32), pltpu.VMEM(shape, jnp.float32)),
        in_specs=[pl.BlockSpec(memory_space=pltpu.HBM)] * 3,
        out_specs=(pl.BlockSpec(memory_space=pltpu.VMEM),) * 2,
        scratch_shapes=[
            pltpu.VMEM(shape, jnp.float32),
            pltpu.VMEM(shape, jnp.float32),
            pltpu.VMEM(shape[1:], jnp.float32),
            pltpu.VMEM(shape, jnp.float32),
            pltpu.SemaphoreType.DMA((2, k)),
            pltpu.SemaphoreType.DMA,
            pltpu.SemaphoreType.DMA((k,)),
            pltpu.SemaphoreType.DMA((k,)),
            pltpu.SemaphoreType.DMA((k, 4)),
            pltpu.SemaphoreType.DMA((k, 3)),
            pltpu.SemaphoreType.DMA,
            pltpu.SemaphoreType.DMA((k,)),
        ],
        compiler_params=pltpu.CompilerParams(
            collective_id=0, has_side_effects=True, vmem_limit_bytes=16 << 20
        ),
        name="exchange",
    )(*(pltpu.with_memory_space_constraint(a.reshape(shape), pltpu.HBM) for a in (momentum, gradient, weights)))
    upd_out, new_w_out = pl.pallas_call(
        put_out,
        out_shape=(jax.ShapeDtypeStruct(shape, jnp.float32),) * 2,
        in_specs=[any_spec] * 2,
        out_specs=(any_spec, any_spec),
        scratch_shapes=[pltpu.SemaphoreType.DMA((2, 4))],
        compiler_params=pltpu.CompilerParams(vmem_limit_bytes=1 << 20),
        name="put_out",
    )(upd, new_w)
    return upd_out.reshape(momentum.shape), new_w_out.reshape(weights.shape)


def solution(mesh):
    return jax.shard_map(
        body,
        mesh=mesh,
        in_specs=(P("worker", "shard"), P("worker", "shard"), P("shard")),
        out_specs=(P("worker", "shard"), P("shard")),
        check_vma=False,
    )
```

```python
import functools

import jax
import jax.numpy as jnp
from jax import lax
from jax.experimental import pallas as pl
from jax.experimental.pallas import tpu as pltpu
from jax.sharding import PartitionSpec as P

MESH = pl.DeviceIdType.MESH
LANES = 128
N = 16
CHUNKS = (64, 64, 64, 64)
NEARS = 2
ROUTES = "xyyY"
STEP = 128
SORT8 = (
    ((0, 2), (1, 3), (4, 6), (5, 7)),
    ((0, 4), (1, 5), (2, 6), (3, 7)),
    ((0, 1), (2, 3), (4, 5), (6, 7)),
    ((2, 4), (3, 5)),
    ((1, 4), (3, 6)),
    ((1, 2), (3, 4), (5, 6)),
)


def sort8(values):
    values = list(values)
    for layer in SORT8:
        for i, j in layer:
            a, b = values[i], values[j]
            values[i], values[j] = jnp.minimum(a, b), jnp.maximum(a, b)
    return values


def trimmed_sum(values):
    a, b = sort8(values[:8]), sort8(values[8:])
    kept = [jnp.maximum(a[i], b[3 - i]) for i in range(4)]
    kept += [jnp.minimum(a[4 + i], b[7 - i]) for i in range(4)]
    while len(kept) > 1:
        kept = [kept[i] + kept[i + 1] for i in range(0, len(kept), 2)]
    return kept[0]


def exchange(m_ref, g_ref, w_ref, upd, new_w, m_buf, g_buf, w_buf, recv,
             round_sem, load_sem, w_sem, out_sem, in_sem, near_sem, far_sem, core_sem, gather_sem):
    me = lax.axis_index("worker")
    x, y, c = me // 8, (me // 2) % 4, me % 2

    def at(dx, dy, dc):
        return ((x + dx) % 2) * 8 + ((y + dy) % 4) * 2 + (c + dc) % 2

    def wait_bytes(ref, sem):
        pltpu.make_async_copy(ref, ref, sem).wait()

    def send(src, dst, s_sem, r_sem, peer):
        pltpu.make_async_remote_copy(
            src_ref=src, dst_ref=dst, send_sem=s_sem, recv_sem=r_sem,
            device_id={"worker": peer}, device_id_type=MESH,
        ).start()

    near = [(1, 0, 0), (1, 0, 1), (0, 1, 0), (0, 3, 0), (0, 1, 1), (0, 3, 1), (0, 0, 1)]
    middle = [(0, 2, 0), (0, 2, 1), (1, 1, 0), (1, 3, 0), (1, 1, 1), (1, 3, 1)]
    last = [(1, 2, 0), (1, 2, 1)]
    ring = [(1, 0, 0), (0, 1, 0), (0, 3, 0)]
    starts = [sum(CHUNKS[:k]) for k in range(len(CHUNKS))]
    spans = [pl.ds(s, r) for s, r in zip(starts, CHUNKS)]
    every = range(len(CHUNKS))

    def signal(sem, o):
        pl.semaphore_signal(sem, inc=1, device_id={"worker": at(*o)}, device_id_type=MESH)

    barrier = pltpu.get_barrier_semaphore()
    for o in near:
        signal(barrier, o)
    order = near + middle + last + [(0, 0, 0)]
    loads = []
    for i, o in enumerate(order):
        block = at(*o)
        pair = (
            pltpu.make_async_copy(m_ref.at[block], m_buf.at[block], load_sem.at[0, i]),
            pltpu.make_async_copy(g_ref.at[block], g_buf.at[block], load_sem.at[1, i]),
        )
        for copy in pair:
            copy.start()
        loads.append(pair)
    w_load = pltpu.make_async_copy(w_ref.at[me], w_buf, w_sem)
    w_load.start()

    def update(i):
        for copy in loads[i]:
            copy.wait()
        block = at(*order[i])

        def one(r, _):
            rows = pl.ds(pl.multiple_of(r * STEP, STEP), STEP)
            upd[block, rows, :] = 0.9 * m_buf[block, rows, :] + g_buf[block, rows, :]
            return 0

        lax.fori_loop(0, upd.shape[1] // STEP, one, 0)

    def scatter(i, k):
        peer = at(*order[i])
        send(upd.at[peer, spans[k]], recv.at[me, spans[k]], out_sem, in_sem.at[k], peer)

    first, second = len(near), len(near) + len(middle)
    update(0)
    for i in range(first):
        update(i + 1)
        if i == 0:
            pl.semaphore_wait(barrier, len(near))
            for o in ring:
                signal(round_sem.at[0], o)
        scatter(i, 0)
    for k in range(1, NEARS):
        for i in range(first):
            scatter(i, k)
    pl.semaphore_wait(round_sem.at[0], len(ring))
    for o in ring:
        signal(round_sem.at[1], o)
    for i in range(first + 1, second + 1):
        update(i)
        scatter(i - 1, 0)
    for i in range(second + 1, len(order)):
        update(i)
    pl.semaphore_wait(round_sem.at[1], len(ring))
    for i in range(second, len(order) - 1):
        scatter(i, 0)
    for k in every[1:]:
        for i in reversed(range(first if k < NEARS else 0, len(order) - 1)):
            scatter(i, k)

    def own(r, _):
        rows = pl.ds(pl.multiple_of(r * 32, 32), 32)
        recv[me, rows, :] = upd[me, rows, :]
        return 0

    lax.fori_loop(0, upd.shape[1] // 32, own, 0)
    w_load.wait()

    other_core, other_x = at(0, 0, 1), at(1, 0, 0)

    sides = ((1, 1), (2, 3))

    def gather(block, k, r_sem, peer):
        part = new_w.at[block, spans[k]]
        send(part, part, gather_sem, r_sem, peer)

    def select(k):
        wait_bytes(recv.at[pl.ds(0, N - 1), spans[k]], in_sem.at[k])

        def one(r, _):
            rows = pl.ds(pl.multiple_of(starts[k] + r * 8, 8), 8)
            total = trimmed_sum([recv[d, rows, :] for d in range(N)])
            new_w[me, rows, :] = w_buf[rows, :] - 0.1 * (total * 0.125)
            return 0

        lax.fori_loop(0, CHUNKS[k] // 8, one, 0)
        gather(me, k, near_sem.at[k, 3], at(0, 2, 0))
        for i, dy in sides:
            gather(me, k, near_sem.at[k, i], at(0, dy, 0))
        gather(me, k, near_sem.at[k, 0], other_x)
        gather(me, k, core_sem, other_core)

    def relay(k):
        wait_bytes(new_w.at[other_x, spans[k]], near_sem.at[k, 0])
        if ROUTES[k] != "x":
            for i, dy in sides:
                gather(other_x, k, far_sem.at[k, i], at(0, dy, 0))
                if ROUTES[k] == "Y":
                    gather(other_x, k, core_sem, at(0, dy, 1))
        gather(other_x, k, core_sem, other_core)
        for i, dy in sides:
            block = at(0, -dy, 0)
            wait_bytes(new_w.at[block, spans[k]], near_sem.at[k, i])
            if ROUTES[k] == "x":
                gather(block, k, far_sem.at[k, i], other_x)
            gather(block, k, core_sem, other_core)
        block = at(0, 2, 0)
        wait_bytes(new_w.at[block, spans[k]], near_sem.at[k, 3])
        gather(block, k, far_sem.at[k, 0], other_x)
        if ROUTES[k] == "Y":
            gather(block, k, core_sem, at(1, 0, 1))
        gather(block, k, core_sem, other_core)

    def relay_far(k):
        for i, dy in (*sides, (0, 2)):
            block = at(1, -dy, 0)
            wait_bytes(new_w.at[block, spans[k]], far_sem.at[k, i])
            if ROUTES[k] != "Y":
                gather(block, k, core_sem, other_core)

    for step in (select, relay, relay_far):
        for k in every:
            step(k)
    wait_bytes(new_w.at[pl.ds(0, 8)], core_sem)
    wait_bytes(recv.at[pl.ds(0, N - 1)], out_sem)
    wait_bytes(recv.at[pl.ds(0, N - 1)], gather_sem)


def put_out(upd, new_w, upd_out, new_w_out, sems):
    parts = sems.shape[1]
    copies = []
    for i, (src, dst) in enumerate(((upd, upd_out), (new_w, new_w_out))):
        for p in range(parts):
            span = pl.ds(p * (N // parts), N // parts)
            copies.append(pltpu.make_async_copy(src.at[span], dst.at[span], sems.at[i, p]))
    for copy in copies:
        copy.start()
    for copy in copies:
        copy.wait()


def body(momentum, gradient, weights):
    rows = momentum.shape[1] // (N * LANES)
    shape = (N, rows, LANES)
    k = len(CHUNKS)
    any_spec = pl.BlockSpec(memory_space=pl.ANY)
    upd, new_w = pl.pallas_call(
        exchange,
        out_shape=(pltpu.VMEM(shape, jnp.float32), pltpu.VMEM(shape, jnp.float32)),
        in_specs=[pl.BlockSpec(memory_space=pltpu.HBM)] * 3,
        out_specs=(pl.BlockSpec(memory_space=pltpu.VMEM),) * 2,
        scratch_shapes=[
            pltpu.VMEM(shape, jnp.float32),
            pltpu.VMEM(shape, jnp.float32),
            pltpu.VMEM(shape[1:], jnp.float32),
            pltpu.VMEM(shape, jnp.float32),
            pltpu.SemaphoreType.REGULAR((2,)),
            pltpu.SemaphoreType.DMA((2, N)),
            pltpu.SemaphoreType.DMA,
            pltpu.SemaphoreType.DMA,
            pltpu.SemaphoreType.DMA((k,)),
            pltpu.SemaphoreType.DMA((k, 4)),
            pltpu.SemaphoreType.DMA((k, 3)),
            pltpu.SemaphoreType.DMA,
            pltpu.SemaphoreType.DMA,
        ],
        compiler_params=pltpu.CompilerParams(
            collective_id=0, has_side_effects=True, vmem_limit_bytes=16 << 20
        ),
        name="exchange",
    )(*(pltpu.with_memory_space_constraint(a.reshape(shape), pltpu.HBM) for a in (momentum, gradient, weights)))
    upd_out, new_w_out = pl.pallas_call(
        put_out,
        out_shape=(jax.ShapeDtypeStruct(shape, jnp.float32),) * 2,
        in_specs=[any_spec] * 2,
        out_specs=(any_spec, any_spec),
        scratch_shapes=[pltpu.SemaphoreType.DMA((2, 1))],
        compiler_params=pltpu.CompilerParams(vmem_limit_bytes=1 << 20),
        name="put_out",
    )(upd, new_w)
    return upd_out.reshape(momentum.shape), new_w_out.reshape(weights.shape)


def solution(mesh):
    return jax.shard_map(
        body,
        mesh=mesh,
        in_specs=(P("worker", "shard"), P("worker", "shard"), P("shard")),
        out_specs=(P("worker", "shard"), P("shard")),
        check_vma=False,
    )
```

```python
import functools

import jax
import jax.numpy as jnp
from jax import lax
from jax.experimental import pallas as pl
from jax.experimental.pallas import tpu as pltpu
from jax.sharding import PartitionSpec as P

MESH = pl.DeviceIdType.MESH
LANES = 128
N = 16
CHUNKS = (80, 64, 64, 48)
NEARS = 1
ROUTES = "xyyY"
GROUPS = (1, 1, 1, 4, 6, 3)
STEP = 128
SORT8 = (
    ((0, 2), (1, 3), (4, 6), (5, 7)),
    ((0, 4), (1, 5), (2, 6), (3, 7)),
    ((0, 1), (2, 3), (4, 5), (6, 7)),
    ((2, 4), (3, 5)),
    ((1, 4), (3, 6)),
    ((1, 2), (3, 4), (5, 6)),
)


def sort8(values):
    values = list(values)
    for layer in SORT8:
        for i, j in layer:
            a, b = values[i], values[j]
            values[i], values[j] = jnp.minimum(a, b), jnp.maximum(a, b)
    return values


def trimmed_sum(values):
    a, b = sort8(values[:8]), sort8(values[8:])
    kept = [jnp.maximum(a[i], b[3 - i]) for i in range(4)]
    kept += [jnp.minimum(a[4 + i], b[7 - i]) for i in range(4)]
    while len(kept) > 1:
        kept = [kept[i] + kept[i + 1] for i in range(0, len(kept), 2)]
    return kept[0]


def exchange(m_ref, g_ref, w_ref, upd, new_w, m_buf, g_buf, w_buf, recv,
             round_sem, load_sem, out_sem, in_sem, near_sem, far_sem, core_sem, gather_sem):
    me = lax.axis_index("worker")
    x, y, c = me // 8, (me // 2) % 4, me % 2

    def at(dx, dy, dc):
        return ((x + dx) % 2) * 8 + ((y + dy) % 4) * 2 + (c + dc) % 2

    def wait_bytes(ref, sem):
        pltpu.make_async_copy(ref, ref, sem).wait()

    def send(src, dst, s_sem, r_sem, peer):
        pltpu.make_async_remote_copy(
            src_ref=src, dst_ref=dst, send_sem=s_sem, recv_sem=r_sem,
            device_id={"worker": peer}, device_id_type=MESH,
        ).start()

    near = [(1, 0, 0), (1, 0, 1), (0, 1, 0), (0, 3, 0), (0, 1, 1), (0, 3, 1), (0, 0, 1)]
    middle = [(0, 2, 0), (0, 2, 1), (1, 1, 0), (1, 3, 0), (1, 1, 1), (1, 3, 1)]
    last = [(1, 2, 0), (1, 2, 1)]
    ring = [(1, 0, 0), (0, 1, 0), (0, 3, 0)]
    starts = [sum(CHUNKS[:k]) for k in range(len(CHUNKS))]
    spans = [pl.ds(s, r) for s, r in zip(starts, CHUNKS)]
    every = range(len(CHUNKS))

    def signal(sem, o):
        pl.semaphore_signal(sem, inc=1, device_id={"worker": at(*o)}, device_id_type=MESH)

    barrier = pltpu.get_barrier_semaphore()
    for o in near:
        signal(barrier, o)
    order = near + middle + last + [(0, 0, 0)]
    group = [g for g, blocks in enumerate(GROUPS) for _ in range(blocks)]
    for i, o in enumerate(order):
        block, sem = at(*o), load_sem.at[group[i]]
        pltpu.make_async_copy(m_ref.at[block], m_buf.at[block], sem).start()
        pltpu.make_async_copy(g_ref.at[block], g_buf.at[block], sem).start()
    pltpu.make_async_copy(w_ref.at[me], w_buf, load_sem.at[group[-1]]).start()

    def update(i):
        if i == 0 or group[i] != group[i - 1]:
            copies = 2 * GROUPS[group[i]] + (group[i] == group[-1])
            wait_bytes(m_buf.at[pl.ds(0, copies)], load_sem.at[group[i]])
        block = at(*order[i])

        def one(r, _):
            rows = pl.ds(pl.multiple_of(r * STEP, STEP), STEP)
            upd[block, rows, :] = 0.9 * m_buf[block, rows, :] + g_buf[block, rows, :]
            return 0

        lax.fori_loop(0, upd.shape[1] // STEP, one, 0)

    def scatter(i, k):
        peer = at(*order[i])
        send(upd.at[peer, spans[k]], recv.at[me, spans[k]], out_sem, in_sem.at[k], peer)

    first, second = len(near), len(near) + len(middle)
    update(0)
    for i in range(first):
        update(i + 1)
        if i == 0:
            pl.semaphore_wait(barrier, len(near))
            for o in ring:
                signal(round_sem.at[0], o)
        scatter(i, 0)
    for k in range(1, NEARS):
        for i in range(first):
            scatter(i, k)
    pl.semaphore_wait(round_sem.at[0], len(ring))
    for o in ring:
        signal(round_sem.at[1], o)
    for i in range(first + 1, second + 1):
        update(i)
        scatter(i - 1, 0)
    for i in range(second + 1, len(order)):
        update(i)
    pl.semaphore_wait(round_sem.at[1], len(ring))
    for i in range(second, len(order) - 1):
        scatter(i, 0)
    for k in every[1:]:
        for i in reversed(range(first if k < NEARS else 0, len(order) - 1)):
            scatter(i, k)

    def own(r, _):
        rows = pl.ds(pl.multiple_of(r * 32, 32), 32)
        recv[me, rows, :] = upd[me, rows, :]
        return 0

    lax.fori_loop(0, upd.shape[1] // 32, own, 0)

    other_core, other_x = at(0, 0, 1), at(1, 0, 0)

    def gather(block, k, r_sem, peer):
        part = new_w.at[block, spans[k]]
        send(part, part, gather_sem, r_sem, peer)

    def wait_blocks(blocks, k, sem):
        wait_bytes(new_w.at[pl.ds(0, blocks), spans[k]], sem)

    def select(k):
        wait_bytes(recv.at[pl.ds(0, N - 1), spans[k]], in_sem.at[k])

        def one(r, _):
            rows = pl.ds(pl.multiple_of(starts[k] + r * 8, 8), 8)
            total = trimmed_sum([recv[d, rows, :] for d in range(N)])
            new_w[me, rows, :] = w_buf[rows, :] - 0.1 * (total * 0.125)
            return 0

        lax.fori_loop(0, CHUNKS[k] // 8, one, 0)
        for dy in (2, 1, 3):
            gather(me, k, near_sem.at[k, 1], at(0, dy, 0))
        gather(me, k, near_sem.at[k, 0], other_x)
        gather(me, k, core_sem, other_core)

    def relay(k):
        wait_blocks(1, k, near_sem.at[k, 0])
        if ROUTES[k] != "x":
            for dy in (1, 3):
                gather(other_x, k, far_sem.at[k], at(0, dy, 0))
                if ROUTES[k] == "Y":
                    gather(other_x, k, core_sem, at(0, dy, 1))
        gather(other_x, k, core_sem, other_core)
        wait_blocks(3, k, near_sem.at[k, 1])
        for dy in (2, 1, 3) if ROUTES[k] == "x" else (2,):
            gather(at(0, dy, 0), k, far_sem.at[k], other_x)
            if ROUTES[k] == "Y":
                gather(at(0, dy, 0), k, core_sem, at(1, 0, 1))
        for dy in (2, 1, 3):
            gather(at(0, dy, 0), k, core_sem, other_core)

    def relay_far(k):
        wait_blocks(3, k, far_sem.at[k])
        for dy in (2, 1, 3) if ROUTES[k] != "Y" else ():
            gather(at(1, dy, 0), k, core_sem, other_core)

    for step in (select, relay, relay_far):
        for k in every:
            step(k)
    wait_bytes(new_w.at[pl.ds(0, 8)], core_sem)
    wait_bytes(recv.at[pl.ds(0, N - 1)], out_sem)
    wait_bytes(recv.at[pl.ds(0, N - 1)], gather_sem)


def put_out(upd, new_w, upd_out, new_w_out, sems):
    parts = sems.shape[1]
    copies = []
    for i, (src, dst) in enumerate(((upd, upd_out), (new_w, new_w_out))):
        for p in range(parts):
            span = pl.ds(p * (N // parts), N // parts)
            copies.append(pltpu.make_async_copy(src.at[span], dst.at[span], sems.at[i, p]))
    for copy in copies:
        copy.start()
    for copy in copies:
        copy.wait()


def body(momentum, gradient, weights):
    rows = momentum.shape[1] // (N * LANES)
    shape = (N, rows, LANES)
    k = len(CHUNKS)
    any_spec = pl.BlockSpec(memory_space=pl.ANY)
    upd, new_w = pl.pallas_call(
        exchange,
        out_shape=(pltpu.VMEM(shape, jnp.float32), pltpu.VMEM(shape, jnp.float32)),
        in_specs=[pl.BlockSpec(memory_space=pltpu.HBM)] * 3,
        out_specs=(pl.BlockSpec(memory_space=pltpu.VMEM),) * 2,
        scratch_shapes=[
            pltpu.VMEM(shape, jnp.float32),
            pltpu.VMEM(shape, jnp.float32),
            pltpu.VMEM(shape[1:], jnp.float32),
            pltpu.VMEM(shape, jnp.float32),
            pltpu.SemaphoreType.REGULAR((2,)),
            pltpu.SemaphoreType.DMA((len(GROUPS),)),
            pltpu.SemaphoreType.DMA,
            pltpu.SemaphoreType.DMA((k,)),
            pltpu.SemaphoreType.DMA((k, 2)),
            pltpu.SemaphoreType.DMA((k,)),
            pltpu.SemaphoreType.DMA,
            pltpu.SemaphoreType.DMA,
        ],
        compiler_params=pltpu.CompilerParams(
            collective_id=0, has_side_effects=True, vmem_limit_bytes=16 << 20
        ),
        name="exchange",
    )(*(pltpu.with_memory_space_constraint(a.reshape(shape), pltpu.HBM) for a in (momentum, gradient, weights)))
    upd_out, new_w_out = pl.pallas_call(
        put_out,
        out_shape=(jax.ShapeDtypeStruct(shape, jnp.float32),) * 2,
        in_specs=[any_spec] * 2,
        out_specs=(any_spec, any_spec),
        scratch_shapes=[pltpu.SemaphoreType.DMA((2, 1))],
        compiler_params=pltpu.CompilerParams(vmem_limit_bytes=1 << 20),
        name="put_out",
    )(upd, new_w)
    return upd_out.reshape(momentum.shape), new_w_out.reshape(weights.shape)


def solution(mesh):
    return jax.shard_map(
        body,
        mesh=mesh,
        in_specs=(P("worker", "shard"), P("worker", "shard"), P("shard")),
        out_specs=(P("worker", "shard"), P("shard")),
        check_vma=False,
    )
```

```python
import functools

import jax
import jax.numpy as jnp
from jax import lax
from jax.experimental import pallas as pl
from jax.experimental.pallas import tpu as pltpu
from jax.sharding import PartitionSpec as P

MESH = pl.DeviceIdType.MESH
LANES = 128
N = 16
CHUNKS = (80, 64, 64, 48)
NEARS = 1
ROUTES = "xyyY"
GROUPS = (1, 1, 1, 4, 6, 3)
STEP = 128
SORT8 = (
    ((0, 2), (1, 3), (4, 6), (5, 7)),
    ((0, 4), (1, 5), (2, 6), (3, 7)),
    ((0, 1), (2, 3), (4, 5), (6, 7)),
    ((2, 4), (3, 5)),
    ((1, 4), (3, 6)),
    ((1, 2), (3, 4), (5, 6)),
)


def sort8(values):
    values = list(values)
    for layer in SORT8:
        for i, j in layer:
            a, b = values[i], values[j]
            values[i], values[j] = jnp.minimum(a, b), jnp.maximum(a, b)
    return values


def trimmed_sum(values):
    a, b = sort8(values[:8]), sort8(values[8:])
    kept = [jnp.maximum(a[i], b[3 - i]) for i in range(4)]
    kept += [jnp.minimum(a[4 + i], b[7 - i]) for i in range(4)]
    while len(kept) > 1:
        kept = [kept[i] + kept[i + 1] for i in range(0, len(kept), 2)]
    return kept[0]


def exchange(m_ref, g_ref, w_ref, upd, new_w, m_buf, g_buf, w_buf, recv,
             round_sem, load_sem, out_sem, in_sem, near_sem, far_sem, core_sem, gather_sem):
    me = lax.axis_index("worker")
    x, y, c = me // 8, (me // 2) % 4, me % 2

    def at(dx, dy, dc):
        return ((x + dx) % 2) * 8 + ((y + dy) % 4) * 2 + (c + dc) % 2

    def wait_bytes(ref, sem):
        pltpu.make_async_copy(ref, ref, sem).wait()

    def send(src, dst, s_sem, r_sem, peer):
        pltpu.make_async_remote_copy(
            src_ref=src, dst_ref=dst, send_sem=s_sem, recv_sem=r_sem,
            device_id={"worker": peer}, device_id_type=MESH,
        ).start()

    near = [(1, 0, 0), (0, 1, 0), (0, 3, 0), (1, 0, 1), (0, 1, 1), (0, 3, 1), (0, 0, 1)]
    middle = [(1, 1, 0), (1, 3, 0), (0, 2, 0), (0, 2, 1), (1, 1, 1), (1, 3, 1)]
    last = [(1, 2, 0), (1, 2, 1)]
    ring = [(1, 0, 0), (0, 1, 0), (0, 3, 0)]
    starts = [sum(CHUNKS[:k]) for k in range(len(CHUNKS))]
    spans = [pl.ds(s, r) for s, r in zip(starts, CHUNKS)]
    every = range(len(CHUNKS))

    def signal(sem, o):
        pl.semaphore_signal(sem, inc=1, device_id={"worker": at(*o)}, device_id_type=MESH)

    barrier = pltpu.get_barrier_semaphore()
    for o in near:
        signal(barrier, o)
    order = near + middle + last + [(0, 0, 0)]
    group = [g for g, blocks in enumerate(GROUPS) for _ in range(blocks)]
    for i, o in enumerate(order):
        block, sem = at(*o), load_sem.at[group[i]]
        pltpu.make_async_copy(m_ref.at[block], m_buf.at[block], sem).start()
        pltpu.make_async_copy(g_ref.at[block], g_buf.at[block], sem).start()
    pltpu.make_async_copy(w_ref.at[me], w_buf, load_sem.at[group[-1]]).start()

    def update(i):
        if i == 0 or group[i] != group[i - 1]:
            copies = 2 * GROUPS[group[i]] + (group[i] == group[-1])
            wait_bytes(m_buf.at[pl.ds(0, copies)], load_sem.at[group[i]])
        block = at(*order[i])

        def one(r, _):
            rows = pl.ds(pl.multiple_of(r * STEP, STEP), STEP)
            upd[block, rows, :] = 0.9 * m_buf[block, rows, :] + g_buf[block, rows, :]
            return 0

        lax.fori_loop(0, upd.shape[1] // STEP, one, 0)

    def scatter(i, k):
        peer = at(*order[i])
        send(upd.at[peer, spans[k]], recv.at[me, spans[k]], out_sem, in_sem.at[k], peer)

    first, second = len(near), len(near) + len(middle)
    update(0)
    for i in range(first):
        update(i + 1)
        if i == 0:
            pl.semaphore_wait(barrier, len(near))
            for o in ring:
                signal(round_sem.at[0], o)
        scatter(i, 0)
    for k in range(1, NEARS):
        for i in range(first):
            scatter(i, k)
    pl.semaphore_wait(round_sem.at[0], len(ring))
    for o in ring:
        signal(round_sem.at[1], o)
    for i in range(first + 1, second + 1):
        update(i)
        scatter(i - 1, 0)
    for i in range(second + 1, len(order)):
        update(i)
    pl.semaphore_wait(round_sem.at[1], len(ring))
    for i in range(second, len(order) - 1):
        scatter(i, 0)
    for k in every[1:]:
        for i in reversed(range(first if k < NEARS else 0, len(order) - 1)):
            scatter(i, k)

    def own(r, _):
        rows = pl.ds(pl.multiple_of(r * 32, 32), 32)
        recv[me, rows, :] = upd[me, rows, :]
        return 0

    lax.fori_loop(0, upd.shape[1] // 32, own, 0)

    other_core, other_x = at(0, 0, 1), at(1, 0, 0)

    def gather(block, k, r_sem, peer):
        part = new_w.at[block, spans[k]]
        send(part, part, gather_sem, r_sem, peer)

    def wait_blocks(blocks, k, sem):
        wait_bytes(new_w.at[pl.ds(0, blocks), spans[k]], sem)

    def select(k):
        wait_bytes(recv.at[pl.ds(0, N - 1), spans[k]], in_sem.at[k])

        def one(r, _):
            rows = pl.ds(pl.multiple_of(starts[k] + r * 8, 8), 8)
            total = trimmed_sum([recv[d, rows, :] for d in range(N)])
            new_w[me, rows, :] = w_buf[rows, :] - 0.1 * (total * 0.125)
            return 0

        lax.fori_loop(0, CHUNKS[k] // 8, one, 0)
        gather(me, k, near_sem.at[k, 0], other_x)
        for dy in (2, 1, 3):
            gather(me, k, near_sem.at[k, 1], at(0, dy, 0))
        gather(me, k, core_sem, other_core)

    def relay(k):
        wait_blocks(1, k, near_sem.at[k, 0])
        if ROUTES[k] != "x":
            for dy in (1, 3):
                gather(other_x, k, far_sem.at[k], at(0, dy, 0))
                if ROUTES[k] == "Y":
                    gather(other_x, k, core_sem, at(0, dy, 1))
        gather(other_x, k, core_sem, other_core)
        wait_blocks(3, k, near_sem.at[k, 1])
        for dy in (2, 1, 3) if ROUTES[k] == "x" else (2,):
            gather(at(0, dy, 0), k, far_sem.at[k], other_x)
            if ROUTES[k] == "Y":
                gather(at(0, dy, 0), k, core_sem, at(1, 0, 1))
        for dy in (2, 1, 3):
            gather(at(0, dy, 0), k, core_sem, other_core)

    def relay_far(k):
        wait_blocks(3, k, far_sem.at[k])
        for dy in (2, 1, 3) if ROUTES[k] != "Y" else ():
            gather(at(1, dy, 0), k, core_sem, other_core)

    for step in (select, relay, relay_far):
        for k in every:
            step(k)
    wait_bytes(new_w.at[pl.ds(0, 8)], core_sem)
    wait_bytes(recv.at[pl.ds(0, N - 1)], out_sem)
    wait_bytes(recv.at[pl.ds(0, N - 1)], gather_sem)


def put_out(upd, new_w, upd_out, new_w_out, sems):
    parts = sems.shape[1]
    copies = []
    for i, (src, dst) in enumerate(((upd, upd_out), (new_w, new_w_out))):
        for p in range(parts):
            span = pl.ds(p * (N // parts), N // parts)
            copies.append(pltpu.make_async_copy(src.at[span], dst.at[span], sems.at[i, p]))
    for copy in copies:
        copy.start()
    for copy in copies:
        copy.wait()


def body(momentum, gradient, weights):
    rows = momentum.shape[1] // (N * LANES)
    shape = (N, rows, LANES)
    k = len(CHUNKS)
    any_spec = pl.BlockSpec(memory_space=pl.ANY)
    upd, new_w = pl.pallas_call(
        exchange,
        out_shape=(pltpu.VMEM(shape, jnp.float32), pltpu.VMEM(shape, jnp.float32)),
        in_specs=[pl.BlockSpec(memory_space=pltpu.HBM)] * 3,
        out_specs=(pl.BlockSpec(memory_space=pltpu.VMEM),) * 2,
        scratch_shapes=[
            pltpu.VMEM(shape, jnp.float32),
            pltpu.VMEM(shape, jnp.float32),
            pltpu.VMEM(shape[1:], jnp.float32),
            pltpu.VMEM(shape, jnp.float32),
            pltpu.SemaphoreType.REGULAR((2,)),
            pltpu.SemaphoreType.DMA((len(GROUPS),)),
            pltpu.SemaphoreType.DMA,
            pltpu.SemaphoreType.DMA((k,)),
            pltpu.SemaphoreType.DMA((k, 2)),
            pltpu.SemaphoreType.DMA((k,)),
            pltpu.SemaphoreType.DMA,
            pltpu.SemaphoreType.DMA,
        ],
        compiler_params=pltpu.CompilerParams(
            collective_id=0, has_side_effects=True, vmem_limit_bytes=16 << 20
        ),
        name="exchange",
    )(*(pltpu.with_memory_space_constraint(a.reshape(shape), pltpu.HBM) for a in (momentum, gradient, weights)))
    upd_out, new_w_out = pl.pallas_call(
        put_out,
        out_shape=(jax.ShapeDtypeStruct(shape, jnp.float32),) * 2,
        in_specs=[any_spec] * 2,
        out_specs=(any_spec, any_spec),
        scratch_shapes=[pltpu.SemaphoreType.DMA((2, 1))],
        compiler_params=pltpu.CompilerParams(vmem_limit_bytes=1 << 20),
        name="put_out",
    )(upd, new_w)
    return upd_out.reshape(momentum.shape), new_w_out.reshape(weights.shape)


def solution(mesh):
    return jax.shard_map(
        body,
        mesh=mesh,
        in_specs=(P("worker", "shard"), P("worker", "shard"), P("shard")),
        out_specs=(P("worker", "shard"), P("shard")),
        check_vma=False,
    )
```
